32 devices in a mesh: group: 2 (over y), frame: 16 (over z, x, core).
Axes of the slice: x: 2, y: 2, z: 4, core: 2. Of those that a mesh axis runs over, the one named last changes fastest.
Arguments:
- queries: bfloat16 [8192, 1536], P(('group', 'frame')), parts along dimension 0, may hold values from -120 to 120, as said below
- key_rows: bfloat16 [8192, 1536], P(('group', 'frame')), parts along dimension 0, may hold values from -6 to 6, as said below
- value_rows: bfloat16 [8192, 1536], P(('group', 'frame')), parts along dimension 0, may hold values from -6 to 6
- out_grad: bfloat16 [8192, 1536], P(('group', 'frame')), parts along dimension 0, may hold values from -6 to 6
- block_mask: int32 [32, 4, 2], P(('group', 'frame')), parts along dimension 0, may hold values 0 or 1
- block_pick: int32 [32, 4], P(('group', 'frame')), parts along dimension 0, may hold values from 0 to 1
Outputs:
- attended: bfloat16 [8192, 1536], P(('group', 'frame')), parts along dimension 0
- query_grad: bfloat16 [8192, 1536], P(('group', 'frame')), parts along dimension 0
- key_grad: bfloat16 [8192, 1536], P(('group', 'frame')), parts along dimension 0
- value_grad: bfloat16 [8192, 1536], P(('group', 'frame')), parts along dimension 0
The draws below stay inside these ranges and needn't reach their ends.
There are 2 independent parts, one for each index of `group`. The reference program is written for one: setup_inputs(seed, part) draws one part's arguments, and reference() takes and returns one part's arrays. A program takes and returns all parts, laid end to end along the dimension named above; each array names one. Nothing has to cross between parts.
Inputs may be any that keep to these rules, and one draw needn't show every extreme that they name: queries of order one; in some draws a few rows are strongly aligned with the keys of two consecutive rows. `key_rows`: keys of order one.
All inputs are finite; a program needn't handle non-finite values. No bound on the sum of `block_mask` on one device may be relied on, other than what follows from the above.
Results may differ from the reference program's by a relative error of at most 0.0054.
Values may be sent and summed in bfloat16 or wider, within the bound.
No kernel may reach another device: no remote copies, remote signals or barrier semaphores. Data moves between devices by JAX's collectives and lax.ppermute only.
A program may use at most 128 MiB of HBM per device.

```python
import jax
import jax.numpy as jnp
from jax import lax

HEADS = 12
HDIM = 128
TOK = 256
BLK = 128
EDGE = 64
FEAT = 1536
NBLK = 2
FRAMES = 16
LEVELS = 4
ROWS = 4096


def key_field(key):
    shape = (FRAMES * TOK, HEADS * HDIM)
    return jnp.clip(jax.random.normal(jax.random.fold_in(key, 31), shape, jnp.float32), -6.0, 6.0)


def draw_key_rows(key, part):
    return key_field(key).astype(jnp.bfloat16)


def draw_queries(key, part):
    shape = (FRAMES * TOK, HEADS * HDIM)
    return jnp.clip(jax.random.normal(jax.random.fold_in(key, 41), shape, jnp.float32), -6.0, 6.0).astype(jnp.bfloat16)


def place_ends(values, stream_key, smallest, largest):
    longest = values.shape.index(max(values.shape))
    spots = []
    for shift in (0, 1):
        where = [jax.random.randint(jax.random.fold_in(stream_key, axis), (), 0, length) for axis, length in enumerate(values.shape)]
        where[longest] = (where[longest] + shift) % values.shape[longest]
        spots.append(tuple(where))
    return values.at[spots[0]].set(smallest).at[spots[1]].set(largest)


def block_levels(rng, extent, split, low, top_value):
    def one(dim, parts):
        draws = jax.random.uniform(jax.random.fold_in(jax.random.fold_in(rng, 6), dim), (parts,), jnp.float32, low / len(split), top_value / len(split))
        return jnp.repeat(jnp.exp(draws), extent[dim] // parts).reshape((-1,) + (1,) * (len(extent) - dim - 1))

    gain = one(*split[0])
    for cut in split[1:]:
        gain = gain * one(*cut)
    return gain


def scatter_about(own_key, shape, width, bound, split=(), kind=jnp.bfloat16):
    entries = width * jax.random.normal(own_key, shape, jnp.float32)
    if split:
        entries = entries * block_levels(own_key, shape, split, -0.22, 0.18)
    return jnp.clip(entries, -bound, bound).astype(kind)


def setup_inputs(seed: int = 0, part: int = 0) -> dict:
    arg_keys = jax.random.split(jax.random.key(seed), 7)
    part_splits = jax.random.split(jax.random.fold_in(arg_keys[6], part), 7)
    queries = draw_queries(jax.random.fold_in(jax.random.fold_in(arg_keys[6], part), 71), part)
    key_rows = draw_key_rows(jax.random.fold_in(jax.random.fold_in(arg_keys[6], part), 71), part)
    value_rows = scatter_about(part_splits[2], (ROWS, FEAT), 1.0, 6.0, ((0, 16),))
    out_grad = scatter_about(part_splits[3], (ROWS, FEAT), 1.0, 6.0, ((0, 16),))
    block_mask = place_ends((jax.random.randint(part_splits[4], (FRAMES, LEVELS, NBLK), 0, 2) < 1).astype(jnp.int32), jax.random.fold_in(part_splits[4], 1), 0, 1)
    block_pick = place_ends(jax.random.randint(part_splits[5], (FRAMES, LEVELS), 0, NBLK), jax.random.fold_in(part_splits[5], 1), 0, NBLK - 1).astype(jnp.int32)
    return dict(queries=queries, key_rows=key_rows, value_rows=value_rows, out_grad=out_grad, block_mask=block_mask, block_pick=block_pick)


def attend_block(query_blk, grad_blk, key_blk, value_blk, valid):
    scale = HDIM ** -0.5
    query_h = query_blk.reshape(query_blk.shape[0], HEADS, HDIM).astype(jnp.float32)
    grad_h = grad_blk.reshape(grad_blk.shape[0], HEADS, HDIM).astype(jnp.float32)
    key_h = key_blk.reshape(key_blk.shape[0], HEADS, HDIM).astype(jnp.float32)
    value_h = value_blk.reshape(value_blk.shape[0], HEADS, HDIM).astype(jnp.float32)
    scores = jnp.einsum("qhd,khd->hqk", query_h, key_h) * scale
    scores = jnp.where(valid[None], scores, -jnp.inf)
    highest = jnp.max(scores, axis=2, keepdims=True)
    weights = jnp.exp(scores - highest)
    weights = weights / jnp.sum(weights, axis=2, keepdims=True)
    rounded = lax.optimization_barrier(weights.astype(jnp.bfloat16)).astype(jnp.float32)
    attended = jnp.einsum("hqk,khd->qhd", rounded, value_h).astype(jnp.bfloat16)
    dprob = jnp.einsum("qhd,khd->hqk", grad_h, value_h)
    inner = jnp.sum(weights * dprob, axis=2, keepdims=True)
    dscore = lax.optimization_barrier((weights * (dprob - inner)).astype(jnp.bfloat16)).astype(jnp.float32)
    query_grad = (jnp.einsum("hqk,khd->qhd", dscore, key_h) * scale).astype(jnp.bfloat16)
    key_term = jnp.einsum("hqk,qhd->khd", dscore, query_h) * scale
    value_term = jnp.einsum("hqk,qhd->khd", rounded, grad_h)
    rows = query_blk.shape[0]
    count = key_blk.shape[0]
    return (attended.reshape(rows, HEADS * HDIM), query_grad.reshape(rows, HEADS * HDIM),
            key_term.reshape(count, HEADS * HDIM), value_term.reshape(count, HEADS * HDIM))


def add_rows(accum, contrib, start):
    current = lax.dynamic_slice_in_dim(accum, start, BLK, 0)
    return lax.dynamic_update_slice_in_dim(accum, current + contrib, start, 0)


def collect(own_terms, low_terms, high_terms, panel_terms, block_pick):
    total = own_terms
    total = total.at[:-1, TOK - EDGE:].add(low_terms[1:].astype(jnp.float32))
    total = total.at[1:, :EDGE].add(high_terms[:-1].astype(jnp.float32))
    frame_ids = jnp.arange(FRAMES, dtype=jnp.int32)
    for bit_level in range(LEVELS):
        partner = jnp.bitwise_xor(frame_ids, 1 << bit_level)
        contrib = panel_terms[partner, bit_level].astype(jnp.float32)
        starts = (block_pick[:, bit_level] * BLK).astype(jnp.int32)
        total = jax.vmap(add_rows)(total, contrib, starts)
    return total.reshape(ROWS, HEADS * HDIM).astype(jnp.bfloat16)


def reference(queries, key_rows, value_rows, out_grad, block_mask, block_pick):
    feat = HEADS * HDIM
    query3 = queries.reshape(FRAMES, TOK, feat)
    grad3 = out_grad.reshape(FRAMES, TOK, feat)
    key3 = key_rows.reshape(FRAMES, TOK, feat)
    value3 = value_rows.reshape(FRAMES, TOK, feat)
    row_block = jnp.arange(TOK, dtype=jnp.int32) // BLK

    def one_frame(frame):
        lower = jnp.maximum(frame - 1, 0)
        upper = jnp.minimum(frame + 1, FRAMES - 1)
        key_parts = [key3[frame], key3[lower][TOK - EDGE:], key3[upper][:EDGE]]
        value_parts = [value3[frame], value3[lower][TOK - EDGE:], value3[upper][:EDGE]]
        valid_parts = [jnp.ones((TOK, TOK), bool),
                       jnp.broadcast_to(frame > 0, (TOK, EDGE)),
                       jnp.broadcast_to(frame < FRAMES - 1, (TOK, EDGE))]
        for bit_level in range(LEVELS):
            partner = jnp.bitwise_xor(frame, 1 << bit_level)
            start = (block_pick[partner, bit_level] * BLK).astype(jnp.int32)
            key_parts.append(lax.dynamic_slice_in_dim(key3[partner], start, BLK, 0))
            value_parts.append(lax.dynamic_slice_in_dim(value3[partner], start, BLK, 0))
            chosen = block_mask[frame, bit_level][row_block]
            valid_parts.append(jnp.broadcast_to(chosen[:, None] > 0, (TOK, BLK)))
        attended, query_grad, key_term, value_term = attend_block(
            query3[frame], grad3[frame], jnp.concatenate(key_parts, 0),
            jnp.concatenate(value_parts, 0), jnp.concatenate(valid_parts, 1))
        low_end = TOK + EDGE
        high_end = TOK + 2 * EDGE
        return (attended, query_grad, key_term[:TOK], value_term[:TOK],
                key_term[TOK:low_end].astype(jnp.bfloat16), value_term[TOK:low_end].astype(jnp.bfloat16),
                key_term[low_end:high_end].astype(jnp.bfloat16), value_term[low_end:high_end].astype(jnp.bfloat16),
                key_term[high_end:].reshape(LEVELS, BLK, feat).astype(jnp.bfloat16),
                value_term[high_end:].reshape(LEVELS, BLK, feat).astype(jnp.bfloat16))

    results = lax.map(one_frame, jnp.arange(FRAMES, dtype=jnp.int32))
    attended = results[0].reshape(ROWS, feat)
    query_grad = results[1].reshape(ROWS, feat)
    key_grad = collect(results[2], results[4], results[6], results[8], block_pick)
    value_grad = collect(results[3], results[5], results[7], results[9], block_pick)
    return (attended, query_grad, key_grad, value_grad)
```

```python
import functools

import jax
import jax.numpy as jnp
from jax import lax
from jax.experimental import pallas as pl
from jax.experimental.pallas import tpu as pltpu
from jax.sharding import PartitionSpec as P

HDIM = 128
BLK = 128
EDGE = 64
SCALE = HDIM ** (-0.5)
LOG2E = 1.4426950408889634
MASKED = -1e30
SPLIT = (6, 6)

F32 = jnp.float32
BF16 = jnp.bfloat16
ANY = pl.BlockSpec(memory_space=pl.ANY)
NT = (((1,), (1,)), ((), ()))
TN = (((0,), (0,)), ((), ()))


def dot(lhs, rhs, dims=(((1,), (0,)), ((), ()))):
    return lax.dot_general(lhs, rhs, dims, preferred_element_type=F32)


def cost(flops, moved, exps=0):
    return pl.CostEstimate(flops=flops, bytes_accessed=moved, transcendentals=exps)


def pack_kernel(rows, col, where_ref, k_ref, v_ref, *rest):
    outs, sem = rest[:-1], rest[-1]
    width = outs[0].shape[2]
    copies = []
    for out, parts in zip(outs, rows, strict=True):
        at = 0
        for index, size in parts:
            start = pl.multiple_of(where_ref[index], EDGE)
            for side, src in enumerate((k_ref, v_ref)):
                copies.append(
                    pltpu.make_async_copy(
                        src.at[pl.ds(start, size), pl.ds(col, width)],
                        out.at[side, pl.ds(at, size)],
                        sem.at[len(copies)],
                    )
                )
            at += size
    for copy in copies:
        copy.start()
    for copy in copies:
        copy.wait()


def pack(where, keys, values, rows, col, width):
    shapes = [
        jax.ShapeDtypeStruct((2, sum(size for _, size in parts), width), BF16) for parts in rows
    ]
    count = 2 * sum(len(parts) for parts in rows)
    return pl.pallas_call(
        functools.partial(pack_kernel, rows, col),
        out_shape=shapes,
        in_specs=[pl.BlockSpec(memory_space=pltpu.SMEM), ANY, ANY],
        out_specs=[ANY] * len(shapes),
        scratch_shapes=[pltpu.SemaphoreType.DMA((count,))],
        compiler_params=pltpu.CompilerParams(vmem_limit_bytes=1 << 20),
        cost_estimate=cost(0, sum(4 * s.size for s in shapes)),
    )(where, keys, values)


def attend_kernel(first, parts, *refs):
    count = len(parts)
    q_ref, g_ref, k_ref, v_ref, bias_ref = refs[:5]
    got = refs[5 : 5 + count]
    refs = refs[5 + count + (0 if first else 2) :]
    o_ref, dq_ref, own_ref = refs[:3]
    back = refs[3 : 3 + count]
    keys, vals = refs[3 + count :]
    tokens = q_ref.shape[0]
    keys[0:tokens] = k_ref[...]
    vals[0:tokens] = v_ref[...]
    at = tokens
    for ref, size in zip(got, parts, strict=True):
        keys[at : at + size] = ref[0]
        vals[at : at + size] = ref[1]
        at += size
    query, grad, key, val = q_ref[...], g_ref[...], keys[...], vals[...]
    blocks = tokens // BLK
    bias = jnp.concatenate(
        [jnp.broadcast_to(bias_ref[b : b + 1], (BLK, at)) for b in range(blocks)], axis=0
    )
    scores = dot(query, key, NT) * (SCALE * LOG2E) + bias
    weights = jnp.exp2(scores - jnp.max(scores, axis=1, keepdims=True))
    weights = weights * (1.0 / jnp.sum(weights, axis=1, keepdims=True))
    rounded = weights.astype(BF16)
    o_ref[...] = dot(rounded, val).astype(BF16)
    dprob = dot(grad, val, NT)
    inner = jnp.sum(weights * dprob, axis=1, keepdims=True)
    dscore = (weights * (dprob - inner)).astype(BF16)
    dq_ref[...] = (dot(dscore, key) * SCALE).astype(BF16)
    terms = (dot(dscore, query, TN) * SCALE, dot(rounded, grad, TN))
    for side, term in enumerate(terms):
        own_ref[side] = term[:tokens]
        at = tokens
        for ref, size in zip(back, parts, strict=True):
            ref[side] = term[at : at + size].astype(BF16)
            at += size


def attend(queries, out_grad, keys, values, bias, got, previous, head, heads):
    tokens, feat = queries.shape
    width = heads * HDIM
    parts = [piece.shape[1] for piece in got]
    total = tokens + sum(parts)
    column = pl.BlockSpec((tokens, HDIM), lambda h: (0, head + h))
    piece_specs = [pl.BlockSpec((2, size, HDIM), lambda h: (0, 0, h)) for size in parts]
    out_shape = [
        jax.ShapeDtypeStruct((tokens, feat), BF16),
        jax.ShapeDtypeStruct((tokens, feat), BF16),
        jax.ShapeDtypeStruct((2, tokens, width), F32),
    ] + [jax.ShapeDtypeStruct((2, size, width), BF16) for size in parts]
    inputs = [queries, out_grad, keys, values, bias, *got]
    specs = [column] * 4 + [pl.BlockSpec(bias.shape, lambda h: (0, 0))] + piece_specs
    aliases = {}
    if previous is not None:
        aliases = {len(inputs): 0, len(inputs) + 1: 1}
        inputs += list(previous)
        specs += [ANY, ANY]
    return pl.pallas_call(
        functools.partial(attend_kernel, previous is None, parts),
        out_shape=out_shape,
        grid=(heads,),
        in_specs=specs,
        out_specs=[column, column, pl.BlockSpec((2, tokens, HDIM), lambda h: (0, 0, h))]
        + piece_specs,
        scratch_shapes=[pltpu.VMEM((total, HDIM), BF16)] * 2,
        input_output_aliases=aliases,
        compiler_params=pltpu.CompilerParams(
            dimension_semantics=("arbitrary",), vmem_limit_bytes=40 << 20
        ),
        cost_estimate=cost(
            12 * tokens * total * width,
            2 * width * (6 * tokens + 4 * tokens + 4 * (total - tokens)),
            tokens * total * heads,
        ),
    )(*inputs)


def combine_kernel(first, rows, where_ref, own_ref, *refs):
    got = refs[: len(rows)]
    refs = refs[len(rows) + (0 if first else 2) :]
    outs, acc = refs[:2], refs[2]
    acc[...] = own_ref[...]
    for ref, parts in zip(got, rows, strict=True):
        at = 0
        for index, size in parts:
            spot = pl.ds(pl.multiple_of(where_ref[index], EDGE), size)
            for side in range(2):
                acc[side, spot] += ref[side, at : at + size].astype(F32)
            at += size
    for side in range(2):
        outs[side][...] = acc[side].astype(BF16)


def combine(where, own, got, rows, previous, head, heads, feat):
    tokens = own.shape[1]
    inputs = [where, own, *got]
    specs = [
        pl.BlockSpec(memory_space=pltpu.SMEM),
        pl.BlockSpec((2, tokens, HDIM), lambda h: (0, 0, h)),
    ] + [pl.BlockSpec((2, piece.shape[1], HDIM), lambda h: (0, 0, h)) for piece in got]
    aliases = {}
    if previous is not None:
        aliases = {len(inputs): 0, len(inputs) + 1: 1}
        inputs += list(previous)
        specs += [ANY, ANY]
    column = pl.BlockSpec((tokens, HDIM), lambda h: (0, head + h))
    return pl.pallas_call(
        functools.partial(combine_kernel, previous is None, rows),
        out_shape=[jax.ShapeDtypeStruct((tokens, feat), BF16)] * 2,
        grid=(heads,),
        in_specs=specs,
        out_specs=[column, column],
        scratch_shapes=[pltpu.VMEM((2, tokens, HDIM), F32)],
        input_output_aliases=aliases,
        compiler_params=pltpu.CompilerParams(
            dimension_semantics=("arbitrary",), vmem_limit_bytes=16 << 20
        ),
        cost_estimate=cost(
            0, sum(2 * piece.size for piece in got) + 6 * own.size
        ),
    )(*inputs)


def per_device(queries, key_rows, value_rows, out_grad, block_mask, block_pick):
    frames = lax.axis_size("frame")
    levels = frames.bit_length() - 1
    device = lax.axis_index("frame")
    tokens, feat = queries.shape
    blocks = tokens // BLK
    odd = device % 2
    where = jnp.concatenate(
        [
            block_pick[0] * BLK,
            jnp.stack([(1 - odd) * (tokens - EDGE), odd * (tokens - EDGE)]).astype(jnp.int32),
        ]
    )
    rows = [[(level, BLK)] for level in range(levels - 1, 0, -1)]
    rows += [[(0, BLK), (levels, EDGE)], [(levels + 1, EDGE)]]
    pairs = [[(f, f ^ (1 << level)) for f in range(frames)] for level in range(levels - 1, -1, -1)]
    beyond = [f + (1 if f % 2 else -1) for f in range(frames)]
    pairs.append([(f, g if 0 <= g < frames else f) for f, g in enumerate(beyond)])

    def bias_of(seen, size):
        return jnp.broadcast_to(jnp.where(seen, 0.0, MASKED).astype(F32)[:, None], (blocks, size))

    mask = block_mask[0] > 0
    always = jnp.ones((blocks,), bool)
    beside = (device > 0) & (device < frames - 1)
    bias = [bias_of(always, tokens)]
    bias += [bias_of(mask[level], BLK) for level in range(levels - 1, -1, -1)]
    bias += [bias_of(always, EDGE), bias_of(always & beside, EDGE)]
    bias = jnp.concatenate(bias, axis=1)

    head = 0
    sent = []
    for heads in SPLIT:
        pieces = pack(where, key_rows, value_rows, rows, head * HDIM, heads * HDIM)
        sent.append([lax.ppermute(p, "frame", to) for p, to in zip(pieces, pairs, strict=True)])
        head += heads
    head = 0
    outs = None
    returned = []
    for heads, got in zip(SPLIT, sent, strict=True):
        attended, query_grad, own, *terms = attend(
            queries, out_grad, key_rows, value_rows, bias, got, outs, head, heads
        )
        outs = (attended, query_grad)
        returned.append(
            (own, [lax.ppermute(t, "frame", to) for t, to in zip(terms, pairs, strict=True)])
        )
        head += heads
    head = 0
    grads = None
    for heads, (own, got) in zip(SPLIT, returned, strict=True):
        grads = combine(where, own, got, rows, grads, head, heads, feat)
        head += heads
    return (*outs, *grads)


def solution(mesh):
    flat = P(("group", "frame"), None)
    return jax.shard_map(
        per_device,
        mesh=mesh,
        in_specs=(flat, flat, flat, flat, P(("group", "frame"), None, None), flat),
        out_specs=(flat, flat, flat, flat),
        check_vma=False,
    )
```

```python
import functools

import jax
import jax.numpy as jnp
from jax import lax
from jax.experimental import pallas as pl
from jax.experimental.pallas import tpu as pltpu
from jax.sharding import PartitionSpec as P

HDIM = 128
BLK = 128
EDGE = 64
SCALE = HDIM ** (-0.5)
LOG2E = 1.4426950408889634
MASKED = -1e30
SPLIT = (6, 6)
PAIR = -1
BEYOND = -2

F32 = jnp.float32
BF16 = jnp.bfloat16
ANY = pl.BlockSpec(memory_space=pl.ANY)
NT = (((1,), (1,)), ((), ()))
TN = (((0,), (0,)), ((), ()))


def dot(lhs, rhs, dims=(((1,), (0,)), ((), ()))):
    return lax.dot_general(lhs, rhs, dims, preferred_element_type=F32)


def hbm(arrays):
    return [pltpu.with_memory_space_constraint(x, pltpu.HBM) for x in arrays]


def vmem(arrays):
    return [pltpu.with_memory_space_constraint(x, pltpu.VMEM) for x in arrays]


def cost(flops, moved, exps=0):
    return pl.CostEstimate(flops=flops, bytes_accessed=moved, transcendentals=exps)


def start_of(kind, pick_ref, tokens):
    odd = lax.axis_index("frame") % 2
    if kind == PAIR:
        return pl.multiple_of((1 - odd) * (tokens - EDGE), EDGE)
    if kind == BEYOND:
        return pl.multiple_of(odd * (tokens - EDGE), EDGE)
    return pl.multiple_of(pick_ref[0, kind] * BLK, BLK)


def pack_kernel(pieces, pick_ref, k_ref, v_ref, *rest):
    outs, sem = rest[:-1], rest[-1]
    copies = []
    for out, (parts, col, width) in zip(outs, pieces, strict=True):
        at = 0
        for kind, size in parts:
            start = start_of(kind, pick_ref, k_ref.shape[0])
            for side, src in enumerate((k_ref, v_ref)):
                copies.append(
                    pltpu.make_async_copy(
                        src.at[pl.ds(start, size), pl.ds(col, width)],
                        out.at[side, pl.ds(at, size)],
                        sem.at[len(copies)],
                    )
                )
            at += size
    for copy in copies:
        copy.start()
    for copy in copies:
        copy.wait()


def pack(picks, keys, values, pieces):
    sizes = [sum(size for _, size in parts) for parts, _, _ in pieces]
    return pl.pallas_call(
        functools.partial(pack_kernel, pieces),
        out_shape=[
            pltpu.VMEM((2, size, width), BF16)
            for size, (_, _, width) in zip(sizes, pieces, strict=True)
        ],
        in_specs=[pl.BlockSpec(memory_space=pltpu.SMEM), ANY, ANY],
        out_specs=[ANY] * len(pieces),
        scratch_shapes=[pltpu.SemaphoreType.DMA((2 * sum(len(parts) for parts, _, _ in pieces),))],
        compiler_params=pltpu.CompilerParams(vmem_limit_bytes=1 << 20),
        cost_estimate=cost(
            0, sum(8 * size * width for size, (_, _, width) in zip(sizes, pieces, strict=True))
        ),
    )(picks, *hbm((keys, values)))


def bias_columns(mask_ref, tokens, blocks, rows):
    frame, frames = lax.axis_index("frame"), lax.axis_size("frame")
    lane = lax.broadcasted_iota(jnp.int32, (1, HDIM), 1)
    pieces = [jnp.zeros((tokens, HDIM), BF16)]
    for parts in rows:
        for kind, size in parts:
            row = jnp.zeros((1, HDIM), F32)
            for b in range(blocks):
                if kind == BEYOND:
                    seen = (frame > 0) & (frame < frames - 1)
                elif kind != PAIR:
                    seen = mask_ref[0, b, kind] > 0
                else:
                    continue
                row = jnp.where(lane == b, jnp.where(seen, 0.0, MASKED), row)
            pieces.append(jnp.broadcast_to(row, (size, HDIM)).astype(BF16))
    return jnp.concatenate(pieces, axis=0)


def attend_kernel(head, heads, rows, aliased, mask_ref, *refs):
    count = len(rows)
    q_ref, g_ref, k_ref, v_ref = refs[:4]
    got = refs[4 : 4 + count]
    refs = refs[4 + count + aliased :]
    o_ref, dq_ref, own_ref = refs[:3]
    back = refs[3 : 3 + count]
    keys, vals = refs[3 + count :]
    tokens = q_ref.shape[0]
    blocks = tokens // BLK
    bias = bias_columns(mask_ref, tokens, blocks, rows)
    for slot in range(2):
        keys[slot, :, HDIM:] = bias
    block = lax.broadcasted_iota(jnp.int32, (tokens, HDIM), 0) // BLK
    lane = lax.broadcasted_iota(jnp.int32, (tokens, HDIM), 1)
    choose = jnp.where(lane == block, 1.0, 0.0).astype(BF16)

    def column(h, ref):
        return pl.ds((h if ref.shape[-1] == heads * HDIM else head + h) * HDIM, HDIM)

    def products(h):
        at = 0
        slot = h % 2
        for ref in (k_ref, v_ref):
            half = keys.at[slot, :, :HDIM] if ref is k_ref else vals.at[slot]
            half[0:tokens] = ref[:, column(h, ref)]
        at = tokens
        for ref in got:
            size = ref.shape[1]
            keys[slot, at : at + size, :HDIM] = ref[0, :, column(h, ref)]
            vals[slot, at : at + size] = ref[1, :, column(h, ref)]
            at += size
        query = jnp.concatenate([q_ref[:, column(h, q_ref)], choose], axis=1)
        return dot(query, keys[slot], NT), dot(g_ref[:, column(h, g_ref)], vals[slot], NT)

    ahead = products(0)
    for h in range(heads):
        scores, dprob = ahead
        if h + 1 < heads:
            ahead = products(h + 1)
        scores = scores * (SCALE * LOG2E)
        weights = jnp.exp2(scores - jnp.max(scores, axis=1, keepdims=True))
        weights = weights * (1.0 / jnp.sum(weights, axis=1, keepdims=True))
        rounded = weights.astype(BF16)
        inner = jnp.sum(weights * dprob, axis=1, keepdims=True)
        dscore = (weights * (dprob - inner)).astype(BF16)
        slot = h % 2
        query, grad = q_ref[:, column(h, q_ref)], g_ref[:, column(h, g_ref)]
        o_ref[:, column(h, o_ref)] = dot(rounded, vals[slot]).astype(BF16)
        dq_ref[:, column(h, dq_ref)] = (dot(dscore, keys[slot, :, :HDIM]) * SCALE).astype(BF16)
        for side, term in enumerate((dot(dscore, query, TN) * SCALE, dot(rounded, grad, TN))):
            own_ref[side, :, column(h, own_ref)] = term[:tokens]
            at = tokens
            for ref in back:
                size = ref.shape[1]
                ref[side, :, column(h, ref)] = term[at : at + size].astype(BF16)
                at += size


def attend(mask, queries, out_grad, keys, values, got, rows, previous, head, heads):
    tokens, feat = queries.shape
    width = heads * HDIM
    sizes = [piece.shape[1] for piece in got]
    total = tokens + sum(sizes)
    inputs = vmem((queries, out_grad, keys, values, *got))
    aliases = {}
    if previous is not None:
        aliases = {1 + len(inputs): 0, 2 + len(inputs): 1}
        inputs += vmem(previous)
    whole = pl.BlockSpec(memory_space=pltpu.VMEM)
    out_shape = [pltpu.VMEM((tokens, feat), BF16)] * 2 + [pltpu.VMEM((2, tokens, width), F32)]
    out_shape += [pltpu.VMEM((2, size, width), BF16) for size in sizes]
    return pl.pallas_call(
        functools.partial(attend_kernel, head, heads, rows, len(aliases)),
        out_shape=out_shape,
        in_specs=[pl.BlockSpec(memory_space=pltpu.SMEM)] + [whole] * len(inputs),
        out_specs=[whole] * len(out_shape),
        scratch_shapes=[
            pltpu.VMEM((2, total, 2 * HDIM), BF16),
            pltpu.VMEM((2, total, HDIM), BF16),
        ],
        input_output_aliases=aliases,
        compiler_params=pltpu.CompilerParams(vmem_limit_bytes=24 << 20),
        cost_estimate=cost(
            12 * tokens * total * width,
            2 * width * (6 * tokens + 4 * tokens + 4 * (total - tokens)),
            tokens * total * heads,
        ),
    )(mask, *inputs)


def combine_kernel(first, rows, pick_ref, own_ref, *refs):
    got = refs[: len(rows)]
    refs = refs[len(rows) + (0 if first else 2) :]
    outs, acc = refs[:2], refs[2]
    acc[...] = own_ref[...]
    for ref, parts in zip(got, rows, strict=True):
        at = 0
        for kind, size in parts:
            spot = pl.ds(start_of(kind, pick_ref, acc.shape[1]), size)
            for side in range(2):
                acc[side, spot] += ref[side, at : at + size].astype(F32)
            at += size
    for side in range(2):
        outs[side][...] = acc[side].astype(BF16)


def combine(picks, own, got, rows, previous, head, heads, feat):
    tokens = own.shape[1]
    inputs = [picks, *vmem((own, *got))]
    specs = [
        pl.BlockSpec(memory_space=pltpu.SMEM),
        pl.BlockSpec((2, tokens, HDIM), lambda h: (0, 0, h)),
    ] + [pl.BlockSpec((2, piece.shape[1], HDIM), lambda h: (0, 0, h)) for piece in got]
    aliases = {}
    if previous is not None:
        aliases = {len(inputs): 0, len(inputs) + 1: 1}
        inputs += hbm(previous)
        specs += [ANY, ANY]
    column = pl.BlockSpec((tokens, HDIM), lambda h: (0, head + h))
    return pl.pallas_call(
        functools.partial(combine_kernel, previous is None, rows),
        out_shape=[pltpu.HBM((tokens, feat), BF16)] * 2,
        grid=(heads,),
        in_specs=specs,
        out_specs=[column, column],
        scratch_shapes=[pltpu.VMEM((2, tokens, HDIM), F32)],
        input_output_aliases=aliases,
        compiler_params=pltpu.CompilerParams(
            dimension_semantics=("arbitrary",), vmem_limit_bytes=16 << 20
        ),
        cost_estimate=cost(
            0, sum(2 * piece.size for piece in got) + 6 * own.size
        ),
    )(*inputs)


def after(pieces, results):
    return [lax.optimization_barrier((piece, *results))[0] for piece in pieces]


def per_device(queries, key_rows, value_rows, out_grad, block_mask, block_pick):
    frames = lax.axis_size("frame")
    levels = frames.bit_length() - 1
    feat = queries.shape[1]
    mask = jnp.swapaxes(block_mask, 1, 2)
    rows = [[(level, BLK)] for level in range(levels - 1, 0, -1)]
    rows += [[(0, BLK), (PAIR, EDGE)], [(BEYOND, EDGE)]]
    pairs = [[(f, f ^ (1 << level)) for f in range(frames)] for level in range(levels - 1, -1, -1)]
    beyond = [f + (1 if f % 2 else -1) for f in range(frames)]
    pairs.append([(f, g if 0 <= g < frames else f) for f, g in enumerate(beyond)])

    def send(pieces, to):
        return [lax.ppermute(piece, "frame", t) for piece, t in zip(pieces, to, strict=True)]

    far = len(rows) - 2
    heads_at = [sum(SPLIT[:i]) for i in range(len(SPLIT))]
    chunks = list(zip(heads_at, SPLIT, strict=True))
    cuts = [[(parts, at * HDIM, n * HDIM) for parts in rows[:far]] for at, n in chunks]
    return_gates = [[far - 1, far]] * far + [[0, far], [0, far + 1]]

    def gated(pieces, before, gates):
        return [
            lax.optimization_barrier((piece, *(before[i] for i in gate)))[0]
            for piece, gate in zip(pieces, gates, strict=True)
        ]

    whole = [(rows[far], 0, feat), (rows[far + 1], 0, feat)]
    *near, = pack(block_pick, key_rows, value_rows, whole + cuts[0])
    first = near[2:]
    edge = send(near[1:2], pairs[far + 1 :])
    fetched = [send(first, pairs[:far])]
    near = send(near[:1], pairs[far : far + 1])
    last = first[:1]
    for cut in cuts[1:]:
        pieces = pack(block_pick, *after((key_rows, value_rows), last), cut)
        last = pieces[:1]
        ready = [fetched[-1][far - 1], *near]
        fetched.append(send(after(pieces, ready), pairs[:far]))
    fetched = [got + near + edge for got in fetched]
    outs = None
    returned = []
    for (head, heads), got in zip(chunks, fetched, strict=True):
        attended, query_grad, own, *terms = attend(
            mask, queries, out_grad, key_rows, value_rows, got, rows, outs, head, heads
        )
        outs = (attended, query_grad)
        if returned:
            terms = gated(terms, returned[-1][1], return_gates)
        returned.append((own, send(terms, pairs)))
    grads = None
    for (head, heads), (own, got) in zip(chunks, returned, strict=True):
        grads = combine(block_pick, own, got, rows, grads, head, heads, feat)
    return (*outs, *grads)


def solution(mesh):
    flat = P(("group", "frame"), None)
    return jax.shard_map(
        per_device,
        mesh=mesh,
        in_specs=(flat, flat, flat, flat, P(("group", "frame"), None, None), flat),
        out_specs=(flat, flat, flat, flat),
        check_vma=False,
    )
```

```python
import functools

import jax
import jax.numpy as jnp
from jax import lax
from jax.experimental import pallas as pl
from jax.experimental.pallas import tpu as pltpu
from jax.sharding import PartitionSpec as P

HDIM = 128
BLK = 128
EDGE = 64
SCALE = HDIM ** (-0.5)
LOG2E = 1.4426950408889634
MASKED = -1e30
SPLIT = (6, 6)
PAIR = -1
BEYOND = -2

F32 = jnp.float32
BF16 = jnp.bfloat16
ANY = pl.BlockSpec(memory_space=pl.ANY)
NT = (((1,), (1,)), ((), ()))
TN = (((0,), (0,)), ((), ()))


def dot(lhs, rhs, dims=(((1,), (0,)), ((), ()))):
    return lax.dot_general(lhs, rhs, dims, preferred_element_type=F32)


def hbm(arrays):
    return [pltpu.with_memory_space_constraint(x, pltpu.HBM) for x in arrays]


def vmem(arrays):
    return [pltpu.with_memory_space_constraint(x, pltpu.VMEM) for x in arrays]


def cost(flops, moved, exps=0):
    return pl.CostEstimate(flops=flops, bytes_accessed=moved, transcendentals=exps)


def start_of(kind, pick_ref, tokens):
    odd = lax.axis_index("frame") % 2
    if kind == PAIR:
        return pl.multiple_of((1 - odd) * (tokens - EDGE), EDGE)
    if kind == BEYOND:
        return pl.multiple_of(odd * (tokens - EDGE), EDGE)
    return pl.multiple_of(pick_ref[0, kind] * BLK, BLK)


def pack_kernel(pieces, pick_ref, k_ref, v_ref, *rest):
    outs, sem = rest[:-1], rest[-1]
    copies = []
    for out, (parts, col, width) in zip(outs, pieces, strict=True):
        at = 0
        for kind, size in parts:
            start = start_of(kind, pick_ref, k_ref.shape[0])
            for side, src in enumerate((k_ref, v_ref)):
                copies.append(
                    pltpu.make_async_copy(
                        src.at[pl.ds(start, size), pl.ds(col, width)],
                        out.at[side, pl.ds(at, size)],
                        sem.at[len(copies)],
                    )
                )
            at += size
    for copy in copies:
        copy.start()
    for copy in copies:
        copy.wait()


def pack(picks, keys, values, pieces):
    sizes = [sum(size for _, size in parts) for parts, _, _ in pieces]
    return pl.pallas_call(
        functools.partial(pack_kernel, pieces),
        out_shape=[
            pltpu.VMEM((2, size, width), BF16)
            for size, (_, _, width) in zip(sizes, pieces, strict=True)
        ],
        in_specs=[pl.BlockSpec(memory_space=pltpu.SMEM), ANY, ANY],
        out_specs=[ANY] * len(pieces),
        scratch_shapes=[pltpu.SemaphoreType.DMA((2 * sum(len(parts) for parts, _, _ in pieces),))],
        compiler_params=pltpu.CompilerParams(vmem_limit_bytes=1 << 20),
        cost_estimate=cost(
            0, sum(8 * size * width for size, (_, _, width) in zip(sizes, pieces, strict=True))
        ),
    )(picks, *hbm((keys, values)))


def bias_columns(mask_ref, tokens, blocks, rows):
    frame, frames = lax.axis_index("frame"), lax.axis_size("frame")
    lane = lax.broadcasted_iota(jnp.int32, (1, HDIM), 1)
    pieces = [jnp.zeros((tokens, HDIM), BF16)]
    for parts in rows:
        for kind, size in parts:
            row = jnp.zeros((1, HDIM), F32)
            for b in range(blocks):
                if kind == BEYOND:
                    seen = (frame > 0) & (frame < frames - 1)
                elif kind != PAIR:
                    seen = mask_ref[0, b, kind] > 0
                else:
                    continue
                row = jnp.where(lane == b, jnp.where(seen, 0.0, MASKED), row)
            pieces.append(jnp.broadcast_to(row, (size, HDIM)).astype(BF16))
    return jnp.concatenate(pieces, axis=0)


def attend_kernel(head, heads, rows, aliased, mask_ref, *refs):
    count = len(rows)
    q_ref, g_ref, k_ref, v_ref = refs[:4]
    got = refs[4 : 4 + count]
    refs = refs[4 + count + aliased :]
    o_ref, dq_ref, own_ref = refs[:3]
    back = refs[3 : 3 + count]
    keys, vals = refs[3 + count :]
    tokens = q_ref.shape[0]
    blocks = tokens // BLK
    bias = bias_columns(mask_ref, tokens, blocks, rows)
    for slot in range(2):
        keys[slot, :, HDIM:] = bias
    block = lax.broadcasted_iota(jnp.int32, (tokens, HDIM), 0) // BLK
    lane = lax.broadcasted_iota(jnp.int32, (tokens, HDIM), 1)
    choose = jnp.where(lane == block, 1.0, 0.0).astype(BF16)

    def column(h, ref):
        return pl.ds((h if ref.shape[-1] == heads * HDIM else head + h) * HDIM, HDIM)

    def products(h):
        at = 0
        slot = h % 2
        for ref in (k_ref, v_ref):
            half = keys.at[slot, :, :HDIM] if ref is k_ref else vals.at[slot]
            half[0:tokens] = ref[:, column(h, ref)]
        at = tokens
        for ref in got:
            size = ref.shape[1]
            keys[slot, at : at + size, :HDIM] = ref[0, :, column(h, ref)]
            vals[slot, at : at + size] = ref[1, :, column(h, ref)]
            at += size
        query = jnp.concatenate([q_ref[:, column(h, q_ref)], choose], axis=1)
        return dot(query, keys[slot], NT), dot(g_ref[:, column(h, g_ref)], vals[slot], NT)

    ahead = products(0)
    for h in range(heads):
        scores, dprob = ahead
        if h + 1 < heads:
            ahead = products(h + 1)
        scores = scores * (SCALE * LOG2E)
        weights = jnp.exp2(scores - jnp.max(scores, axis=1, keepdims=True))
        weights = weights * (1.0 / jnp.sum(weights, axis=1, keepdims=True))
        rounded = weights.astype(BF16)
        inner = jnp.sum(weights * dprob, axis=1, keepdims=True)
        dscore = (weights * (dprob - inner)).astype(BF16)
        slot = h % 2
        query, grad = q_ref[:, column(h, q_ref)], g_ref[:, column(h, g_ref)]
        o_ref[:, column(h, o_ref)] = dot(rounded, vals[slot]).astype(BF16)
        dq_ref[:, column(h, dq_ref)] = (dot(dscore, keys[slot, :, :HDIM]) * SCALE).astype(BF16)
        for side, term in enumerate((dot(dscore, query, TN) * SCALE, dot(rounded, grad, TN))):
            own_ref[side, :, column(h, own_ref)] = term[:tokens]
            at = tokens
            for ref in back:
                size = ref.shape[1]
                ref[side, :, column(h, ref)] = term[at : at + size].astype(BF16)
                at += size


def attend(mask, queries, out_grad, keys, values, got, rows, previous, head, heads):
    tokens, feat = queries.shape
    width = heads * HDIM
    sizes = [piece.shape[1] for piece in got]
    total = tokens + sum(sizes)
    inputs = vmem((queries, out_grad, keys, values, *got))
    aliases = {}
    if previous is not None:
        aliases = {1 + len(inputs): 0, 2 + len(inputs): 1}
        inputs += vmem(previous)
    whole = pl.BlockSpec(memory_space=pltpu.VMEM)
    out_shape = [pltpu.VMEM((tokens, feat), BF16)] * 2 + [pltpu.VMEM((2, tokens, width), F32)]
    out_shape += [pltpu.VMEM((2, size, width), BF16) for size in sizes]
    return pl.pallas_call(
        functools.partial(attend_kernel, head, heads, rows, len(aliases)),
        out_shape=out_shape,
        in_specs=[pl.BlockSpec(memory_space=pltpu.SMEM)] + [whole] * len(inputs),
        out_specs=[whole] * len(out_shape),
        scratch_shapes=[
            pltpu.VMEM((2, total, 2 * HDIM), BF16),
            pltpu.VMEM((2, total, HDIM), BF16),
        ],
        input_output_aliases=aliases,
        compiler_params=pltpu.CompilerParams(vmem_limit_bytes=24 << 20),
        cost_estimate=cost(
            12 * tokens * total * width,
            2 * width * (6 * tokens + 4 * tokens + 4 * (total - tokens)),
            tokens * total * heads,
        ),
    )(mask, *inputs)


def combine_kernel(head, heads, rows, aliased, pick_ref, own_ref, *refs):
    got = refs[: len(rows)]
    refs = refs[len(rows) + aliased :]
    outs, acc, done, sem = refs[:2], refs[2], refs[3], refs[4]
    tokens = own_ref.shape[1]
    starts = [[start_of(kind, pick_ref, tokens) for kind, _ in parts] for parts in rows]
    copies = []
    for side in range(2):
        acc[...] = own_ref[side]
        for ref, parts, spots in zip(got, rows, starts, strict=True):
            at = 0
            cut = slice(None) if ref.shape[2] == heads * HDIM else slice(head * HDIM, (head + heads) * HDIM)
            for (_, size), start in zip(parts, spots, strict=True):
                acc[pl.ds(start, size)] += ref[side, at : at + size, cut].astype(F32)
                at += size
        done[side] = acc[...].astype(BF16)
        target = outs[side].at[:, pl.ds(head * HDIM, heads * HDIM)]
        copies.append(pltpu.make_async_copy(done.at[side], target, sem.at[side]))
        copies[-1].start()
    for copy in copies:
        copy.wait()


def combine(picks, own, got, rows, previous, head, heads, feat):
    tokens = own.shape[1]
    inputs = vmem((own, *got))
    specs = [pl.BlockSpec(memory_space=pltpu.VMEM)] * len(inputs)
    aliases = {}
    if previous is not None:
        aliases = {1 + len(inputs): 0, 2 + len(inputs): 1}
        inputs += hbm(previous)
        specs += [ANY, ANY]
    return pl.pallas_call(
        functools.partial(combine_kernel, head, heads, rows, len(aliases)),
        out_shape=[pltpu.HBM((tokens, feat), BF16)] * 2,
        in_specs=[pl.BlockSpec(memory_space=pltpu.SMEM)] + specs,
        out_specs=[ANY, ANY],
        scratch_shapes=[
            pltpu.VMEM((tokens, heads * HDIM), F32),
            pltpu.VMEM((2, tokens, heads * HDIM), BF16),
            pltpu.SemaphoreType.DMA((2,)),
        ],
        input_output_aliases=aliases,
        compiler_params=pltpu.CompilerParams(vmem_limit_bytes=8 << 20),
        cost_estimate=cost(0, 8 * own.size),
    )(picks, *inputs)


def after(pieces, results):
    return [lax.optimization_barrier((piece, *results))[0] for piece in pieces]


def per_device(queries, key_rows, value_rows, out_grad, block_mask, block_pick):
    frames = lax.axis_size("frame")
    levels = frames.bit_length() - 1
    feat = queries.shape[1]
    mask = jnp.swapaxes(block_mask, 1, 2)
    rows = [[(level, BLK)] for level in range(levels - 1, 0, -1)]
    rows += [[(0, BLK), (PAIR, EDGE)], [(BEYOND, EDGE)]]
    pairs = [[(f, f ^ (1 << level)) for f in range(frames)] for level in range(levels - 1, -1, -1)]
    beyond = [f + (1 if f % 2 else -1) for f in range(frames)]
    pairs.append([(f, g if 0 <= g < frames else f) for f, g in enumerate(beyond)])

    def send(pieces, to):
        return [lax.ppermute(piece, "frame", t) for piece, t in zip(pieces, to, strict=True)]

    far = len(rows) - 2
    heads_at = [sum(SPLIT[:i]) for i in range(len(SPLIT))]
    chunks = list(zip(heads_at, SPLIT, strict=True))
    cuts = [[(parts, at * HDIM, n * HDIM) for parts in rows[:far]] for at, n in chunks]
    return_gates = [[0]] + [[]] * (far - 1) + [[0, 1, far + 1], [1, far - 1, far]]

    def gated(pieces, before, gates):
        return [
            lax.optimization_barrier((piece, *(before[i] for i in gate)))[0]
            for piece, gate in zip(pieces, gates, strict=True)
        ]

    whole = [(rows[far], 0, feat), (rows[far + 1], 0, feat)]
    *near, = pack(block_pick, key_rows, value_rows, whole + cuts[0])
    first = near[2:]
    edge = send(near[1:2], pairs[far + 1 :])
    fetched = [send(first, pairs[:far])]
    near = send(near[:1], pairs[far : far + 1])
    last = first[:1]
    for cut in cuts[1:]:
        *pieces, = pack(block_pick, *after((key_rows, value_rows), last), cut)
        last = pieces[:1]
        before = fetched[-1]
        gates = [[before[0], *near] for i in range(far)]
        pieces = [after([p], gate)[0] for p, gate in zip(pieces, gates, strict=True)]
        fetched.append(send(pieces, pairs[:far]))
    fetched = [got + near + edge for got in fetched]
    outs = None
    returned = []
    for (head, heads), got in zip(chunks, fetched, strict=True):
        attended, query_grad, own, *terms = attend(
            mask, queries, out_grad, key_rows, value_rows, got, rows, outs, head, heads
        )
        outs = (attended, query_grad)
        if returned:
            terms = gated(terms, returned[-1][1], return_gates)
        returned.append((own, send(terms, pairs)))
    grads = None
    for (head, heads), (own, got) in zip(chunks, returned, strict=True):
        grads = combine(block_pick, own, got, rows, grads, head, heads, feat)
    return (*outs, *grads)


def solution(mesh):
    flat = P(("group", "frame"), None)
    return jax.shard_map(
        per_device,
        mesh=mesh,
        in_specs=(flat, flat, flat, flat, P(("group", "frame"), None, None), flat),
        out_specs=(flat, flat, flat, flat),
        check_vma=False,
    )
```

```python
import functools

import jax
import jax.numpy as jnp
from jax import lax
from jax.experimental import pallas as pl
from jax.experimental.pallas import tpu as pltpu
from jax.sharding import PartitionSpec as P

HDIM = 128
BLK = 128
EDGE = 64
SCALE = HDIM ** (-0.5)
LOG2E = 1.4426950408889634
MASKED = -1e30
SPLIT = (6, 6)
PAIR = -1
BEYOND = -2

F32 = jnp.float32
BF16 = jnp.bfloat16
ANY = pl.BlockSpec(memory_space=pl.ANY)
NT = (((1,), (1,)), ((), ()))
TN = (((0,), (0,)), ((), ()))


def dot(lhs, rhs, dims=(((1,), (0,)), ((), ()))):
    return lax.dot_general(lhs, rhs, dims, preferred_element_type=F32)


def hbm(arrays):
    return [pltpu.with_memory_space_constraint(x, pltpu.HBM) for x in arrays]


def vmem(arrays):
    return [pltpu.with_memory_space_constraint(x, pltpu.VMEM) for x in arrays]


def cost(flops, moved, exps=0):
    return pl.CostEstimate(flops=flops, bytes_accessed=moved, transcendentals=exps)


def start_of(kind, pick_ref, tokens):
    odd = lax.axis_index("frame") % 2
    if kind == PAIR:
        return pl.multiple_of((1 - odd) * (tokens - EDGE), EDGE)
    if kind == BEYOND:
        return pl.multiple_of(odd * (tokens - EDGE), EDGE)
    return pl.multiple_of(pick_ref[0, kind] * BLK, BLK)


def pack_kernel(pieces, pick_ref, k_ref, v_ref, *rest):
    outs, sem = rest[:-1], rest[-1]
    copies = []
    for out, (parts, col, width) in zip(outs, pieces, strict=True):
        at = 0
        for kind, size in parts:
            start = start_of(kind, pick_ref, k_ref.shape[0])
            for side, src in enumerate((k_ref, v_ref)):
                copies.append(
                    pltpu.make_async_copy(
                        src.at[pl.ds(start, size), pl.ds(col, width)],
                        out.at[side, pl.ds(at, size)],
                        sem.at[len(copies)],
                    )
                )
            at += size
    for copy in copies:
        copy.start()
    for copy in copies:
        copy.wait()


def pack(picks, keys, values, pieces):
    sizes = [sum(size for _, size in parts) for parts, _, _ in pieces]
    return pl.pallas_call(
        functools.partial(pack_kernel, pieces),
        out_shape=[
            pltpu.VMEM((2, size, width), BF16)
            for size, (_, _, width) in zip(sizes, pieces, strict=True)
        ],
        in_specs=[pl.BlockSpec(memory_space=pltpu.SMEM), ANY, ANY],
        out_specs=[ANY] * len(pieces),
        scratch_shapes=[pltpu.SemaphoreType.DMA((2 * sum(len(parts) for parts, _, _ in pieces),))],
        compiler_params=pltpu.CompilerParams(vmem_limit_bytes=1 << 20),
        cost_estimate=cost(
            0, sum(8 * size * width for size, (_, _, width) in zip(sizes, pieces, strict=True))
        ),
    )(picks, *hbm((keys, values)))


def bias_columns(mask_ref, tokens, blocks, rows):
    frame, frames = lax.axis_index("frame"), lax.axis_size("frame")
    lane = lax.broadcasted_iota(jnp.int32, (1, HDIM), 1)
    pieces = [jnp.zeros((tokens, HDIM), BF16)]
    for parts in rows:
        for kind, size in parts:
            row = jnp.zeros((1, HDIM), F32)
            for b in range(blocks):
                if kind == BEYOND:
                    seen = (frame > 0) & (frame < frames - 1)
                elif kind != PAIR:
                    seen = mask_ref[0, b, kind] > 0
                else:
                    continue
                row = jnp.where(lane == b, jnp.where(seen, 0.0, MASKED), row)
            pieces.append(jnp.broadcast_to(row, (size, HDIM)).astype(BF16))
    return jnp.concatenate(pieces, axis=0)


def attend_kernel(head, heads, rows, aliased, mask_ref, *refs):
    count = len(rows)
    q_ref, g_ref, k_ref, v_ref = refs[:4]
    got = refs[4 : 4 + count]
    refs = refs[4 + count + aliased :]
    o_ref, dq_ref, own_ref = refs[:3]
    back = refs[3 : 3 + count]
    keys, vals = refs[3 + count :]
    tokens = q_ref.shape[0]
    blocks = tokens // BLK
    bias = bias_columns(mask_ref, tokens, blocks, rows)
    for slot in range(2):
        keys[slot, :, HDIM:] = bias
    block = lax.broadcasted_iota(jnp.int32, (tokens, HDIM), 0) // BLK
    lane = lax.broadcasted_iota(jnp.int32, (tokens, HDIM), 1)
    choose = jnp.where(lane == block, 1.0, 0.0).astype(BF16)

    def column(h, ref):
        return pl.ds((h if ref.shape[-1] == heads * HDIM else head + h) * HDIM, HDIM)

    def products(h):
        at = 0
        slot = h % 2
        for ref in (k_ref, v_ref):
            half = keys.at[slot, :, :HDIM] if ref is k_ref else vals.at[slot]
            half[0:tokens] = ref[:, column(h, ref)]
        at = tokens
        for ref in got:
            size = ref.shape[1]
            keys[slot, at : at + size, :HDIM] = ref[0, :, column(h, ref)]
            vals[slot, at : at + size] = ref[1, :, column(h, ref)]
            at += size
        query = jnp.concatenate([q_ref[:, column(h, q_ref)], choose], axis=1)
        return dot(query, keys[slot], NT), dot(g_ref[:, column(h, g_ref)], vals[slot], NT)

    ahead = products(0)
    for h in range(heads):
        scores, dprob = ahead
        if h + 1 < heads:
            ahead = products(h + 1)
        scores = scores * (SCALE * LOG2E)
        weights = jnp.exp2(scores - jnp.max(scores, axis=1, keepdims=True))
        weights = weights * (1.0 / jnp.sum(weights, axis=1, keepdims=True))
        rounded = weights.astype(BF16)
        inner = jnp.sum(weights * dprob, axis=1, keepdims=True)
        dscore = (weights * (dprob - inner)).astype(BF16)
        slot = h % 2
        query, grad = q_ref[:, column(h, q_ref)], g_ref[:, column(h, g_ref)]
        o_ref[:, column(h, o_ref)] = dot(rounded, vals[slot]).astype(BF16)
        dq_ref[:, column(h, dq_ref)] = (dot(dscore, keys[slot, :, :HDIM]) * SCALE).astype(BF16)
        for side, term in enumerate((dot(dscore, query, TN) * SCALE, dot(rounded, grad, TN))):
            own_ref[side, :, column(h, own_ref)] = term[:tokens]
            at = tokens
            for ref in back:
                size = ref.shape[1]
                ref[side, :, column(h, ref)] = term[at : at + size].astype(BF16)
                at += size


def attend(mask, queries, out_grad, keys, values, got, rows, previous, head, heads):
    tokens, feat = queries.shape
    width = heads * HDIM
    sizes = [piece.shape[1] for piece in got]
    total = tokens + sum(sizes)
    inputs = vmem((queries, out_grad, keys, values, *got))
    aliases = {}
    if previous is not None:
        aliases = {1 + len(inputs): 0, 2 + len(inputs): 1}
        inputs += vmem(previous)
    whole = pl.BlockSpec(memory_space=pltpu.VMEM)
    out_shape = [pltpu.VMEM((tokens, feat), BF16)] * 2 + [pltpu.VMEM((2, tokens, width), F32)]
    out_shape += [pltpu.VMEM((2, size, width), BF16) for size in sizes]
    return pl.pallas_call(
        functools.partial(attend_kernel, head, heads, rows, len(aliases)),
        out_shape=out_shape,
        in_specs=[pl.BlockSpec(memory_space=pltpu.SMEM)] + [whole] * len(inputs),
        out_specs=[whole] * len(out_shape),
        scratch_shapes=[
            pltpu.VMEM((2, total, 2 * HDIM), BF16),
            pltpu.VMEM((2, total, HDIM), BF16),
        ],
        input_output_aliases=aliases,
        compiler_params=pltpu.CompilerParams(vmem_limit_bytes=24 << 20),
        cost_estimate=cost(
            12 * tokens * total * width,
            2 * width * (6 * tokens + 4 * tokens + 4 * (total - tokens)),
            tokens * total * heads,
        ),
    )(mask, *inputs)


def combine_kernel(head, heads, rows, aliased, pick_ref, own_ref, *refs):
    got = refs[: len(rows)]
    refs = refs[len(rows) + aliased :]
    outs, acc, done, sem = refs[:2], refs[2], refs[3], refs[4]
    tokens = own_ref.shape[1]
    starts = [[start_of(kind, pick_ref, tokens) for kind, _ in parts] for parts in rows]
    copies = []
    for side in range(2):
        acc[...] = own_ref[side]
        for ref, parts, spots in zip(got, rows, starts, strict=True):
            at = 0
            cut = slice(None) if ref.shape[2] == heads * HDIM else slice(head * HDIM, (head + heads) * HDIM)
            for (_, size), start in zip(parts, spots, strict=True):
                acc[pl.ds(start, size)] += ref[side, at : at + size, cut].astype(F32)
                at += size
        done[side] = acc[...].astype(BF16)
        target = outs[side].at[:, pl.ds(head * HDIM, heads * HDIM)]
        copies.append(pltpu.make_async_copy(done.at[side], target, sem.at[side]))
        copies[-1].start()
    for copy in copies:
        copy.wait()


def combine(picks, own, got, rows, previous, head, heads, feat):
    tokens = own.shape[1]
    inputs = vmem((own, *got))
    specs = [pl.BlockSpec(memory_space=pltpu.VMEM)] * len(inputs)
    aliases = {}
    if previous is not None:
        aliases = {1 + len(inputs): 0, 2 + len(inputs): 1}
        inputs += hbm(previous)
        specs += [ANY, ANY]
    return pl.pallas_call(
        functools.partial(combine_kernel, head, heads, rows, len(aliases)),
        out_shape=[pltpu.HBM((tokens, feat), BF16)] * 2,
        in_specs=[pl.BlockSpec(memory_space=pltpu.SMEM)] + specs,
        out_specs=[ANY, ANY],
        scratch_shapes=[
            pltpu.VMEM((tokens, heads * HDIM), F32),
            pltpu.VMEM((2, tokens, heads * HDIM), BF16),
            pltpu.SemaphoreType.DMA((2,)),
        ],
        input_output_aliases=aliases,
        compiler_params=pltpu.CompilerParams(vmem_limit_bytes=8 << 20),
        cost_estimate=cost(0, 8 * own.size),
    )(picks, *inputs)


def after(pieces, results):
    return [lax.optimization_barrier((piece, *results))[0] for piece in pieces]


def per_device(queries, key_rows, value_rows, out_grad, block_mask, block_pick):
    frames = lax.axis_size("frame")
    levels = frames.bit_length() - 1
    feat = queries.shape[1]
    mask = jnp.swapaxes(block_mask, 1, 2)
    rows = [[(level, BLK)] for level in range(levels - 1, 0, -1)]
    rows += [[(0, BLK), (PAIR, EDGE)], [(BEYOND, EDGE)]]
    pairs = [[(f, f ^ (1 << level)) for f in range(frames)] for level in range(levels - 1, -1, -1)]
    beyond = [f + (1 if f % 2 else -1) for f in range(frames)]
    pairs.append([(f, g if 0 <= g < frames else f) for f, g in enumerate(beyond)])

    def send(pieces, to):
        return [lax.ppermute(piece, "frame", t) for piece, t in zip(pieces, to, strict=True)]

    far = len(rows) - 2
    heads_at = [sum(SPLIT[:i]) for i in range(len(SPLIT))]
    chunks = list(zip(heads_at, SPLIT, strict=True))
    cuts = [[(parts, at * HDIM, n * HDIM) for parts in rows[:far]] for at, n in chunks]
    return_gates = [[]] * far + [[far], [*range(far + 1)]]

    def gated(pieces, before, gates):
        return [
            lax.optimization_barrier((piece, *(before[i] for i in gate)))[0]
            for piece, gate in zip(pieces, gates, strict=True)
        ]

    whole = [(rows[far], 0, feat), (rows[far + 1], 0, feat)]
    *near, = pack(block_pick, key_rows, value_rows, whole + cuts[0])
    first = near[2:]
    edge = send(near[1:2], pairs[far + 1 :])
    fetched = [send(first, pairs[:far])]
    near = send(near[:1], pairs[far : far + 1])
    last = first[:1]
    for cut in cuts[1:]:
        *pieces, = pack(block_pick, *after((key_rows, value_rows), last), cut)
        last = pieces[:1]
        before = fetched[-1]
        gates = [[before[0], *near] for i in range(far)]
        pieces = [after([p], gate)[0] for p, gate in zip(pieces, gates, strict=True)]
        fetched.append(send(pieces, pairs[:far]))
    fetched = [got + near + edge for got in fetched]
    outs = None
    returned = []
    for (head, heads), got in zip(chunks, fetched, strict=True):
        attended, query_grad, own, *terms = attend(
            mask, queries, out_grad, key_rows, value_rows, got, rows, outs, head, heads
        )
        outs = (attended, query_grad)
        if returned:
            terms = gated(terms, returned[-1][1], return_gates)
        returned.append((own, send(terms, pairs)))
    grads = None
    for (head, heads), (own, got) in zip(chunks, returned, strict=True):
        grads = combine(block_pick, own, got, rows, grads, head, heads, feat)
    return (*outs, *grads)


def solution(mesh):
    flat = P(("group", "frame"), None)
    return jax.shard_map(
        per_device,
        mesh=mesh,
        in_specs=(flat, flat, flat, flat, P(("group", "frame"), None, None), flat),
        out_specs=(flat, flat, flat, flat),
        check_vma=False,
    )
```

```python
import functools

import jax
import jax.numpy as jnp
from jax import lax
from jax.experimental import pallas as pl
from jax.experimental.pallas import tpu as pltpu
from jax.sharding import PartitionSpec as P

HDIM = 128
BLK = 128
EDGE = 64
SCALE = HDIM ** (-0.5)
LOG2E = 1.4426950408889634
MASKED = -1e30
SPLIT = (6, 6)
PAIR = -1
BEYOND = -2

F32 = jnp.float32
BF16 = jnp.bfloat16
ANY = pl.BlockSpec(memory_space=pl.ANY)
NT = (((1,), (1,)), ((), ()))
TN = (((0,), (0,)), ((), ()))


def dot(lhs, rhs, dims=(((1,), (0,)), ((), ()))):
    return lax.dot_general(lhs, rhs, dims, preferred_element_type=F32)


def hbm(arrays):
    return [pltpu.with_memory_space_constraint(x, pltpu.HBM) for x in arrays]


def vmem(arrays):
    return [pltpu.with_memory_space_constraint(x, pltpu.VMEM) for x in arrays]


def cost(flops, moved, exps=0):
    return pl.CostEstimate(flops=flops, bytes_accessed=moved, transcendentals=exps)


def start_of(kind, pick_ref, tokens):
    odd = lax.axis_index("frame") % 2
    if kind == PAIR:
        return pl.multiple_of((1 - odd) * (tokens - EDGE), EDGE)
    if kind == BEYOND:
        return pl.multiple_of(odd * (tokens - EDGE), EDGE)
    return pl.multiple_of(pick_ref[0, kind] * BLK, BLK)


def pack_kernel(pieces, pick_ref, k_ref, v_ref, *rest):
    outs, sem = rest[:-1], rest[-1]
    copies = []
    for out, (parts, col, width) in zip(outs, pieces, strict=True):
        at = 0
        for kind, size in parts:
            start = start_of(kind, pick_ref, k_ref.shape[0])
            for side, src in enumerate((k_ref, v_ref)):
                copies.append(
                    pltpu.make_async_copy(
                        src.at[pl.ds(start, size), pl.ds(col, width)],
                        out.at[side, pl.ds(at, size)],
                        sem.at[len(copies)],
                    )
                )
            at += size
    for copy in copies:
        copy.start()
    for copy in copies:
        copy.wait()


def pack(picks, keys, values, pieces):
    sizes = [sum(size for _, size in parts) for parts, _, _ in pieces]
    return pl.pallas_call(
        functools.partial(pack_kernel, pieces),
        out_shape=[
            pltpu.VMEM((2, size, width), BF16)
            for size, (_, _, width) in zip(sizes, pieces, strict=True)
        ],
        in_specs=[pl.BlockSpec(memory_space=pltpu.SMEM), ANY, ANY],
        out_specs=[ANY] * len(pieces),
        scratch_shapes=[pltpu.SemaphoreType.DMA((2 * sum(len(parts) for parts, _, _ in pieces),))],
        compiler_params=pltpu.CompilerParams(vmem_limit_bytes=1 << 20),
        cost_estimate=cost(
            0, sum(8 * size * width for size, (_, _, width) in zip(sizes, pieces, strict=True))
        ),
    )(picks, *hbm((keys, values)))


def bias_columns(mask_ref, tokens, blocks, rows):
    frame, frames = lax.axis_index("frame"), lax.axis_size("frame")
    lane = lax.broadcasted_iota(jnp.int32, (1, HDIM), 1)
    pieces = [jnp.zeros((tokens, HDIM), BF16)]
    for parts in rows:
        for kind, size in parts:
            row = jnp.zeros((1, HDIM), F32)
            for b in range(blocks):
                if kind == BEYOND:
                    seen = (frame > 0) & (frame < frames - 1)
                elif kind != PAIR:
                    seen = mask_ref[0, b, kind] > 0
                else:
                    continue
                row = jnp.where(lane == b, jnp.where(seen, 0.0, MASKED), row)
            pieces.append(jnp.broadcast_to(row, (size, HDIM)).astype(BF16))
    return jnp.concatenate(pieces, axis=0)


def attend_kernel(head, heads, rows, aliased, mask_ref, *refs):
    count = len(rows)
    q_ref, g_ref, k_ref, v_ref = refs[:4]
    got = refs[4 : 4 + count]
    refs = refs[4 + count + aliased :]
    o_ref, dq_ref, own_ref = refs[:3]
    back = refs[3 : 3 + count]
    keys, vals = refs[3 + count :]
    tokens = q_ref.shape[0]
    blocks = tokens // BLK
    bias = bias_columns(mask_ref, tokens, blocks, rows)
    for slot in range(2):
        keys[slot, :, HDIM:] = bias
    block = lax.broadcasted_iota(jnp.int32, (tokens, HDIM), 0) // BLK
    lane = lax.broadcasted_iota(jnp.int32, (tokens, HDIM), 1)
    choose = jnp.where(lane == block, 1.0, 0.0).astype(BF16)

    def column(h, ref):
        return pl.ds((h if ref.shape[-1] == heads * HDIM else head + h) * HDIM, HDIM)

    def products(h):
        at = 0
        slot = h % 2
        for ref in (k_ref, v_ref):
            half = keys.at[slot, :, :HDIM] if ref is k_ref else vals.at[slot]
            half[0:tokens] = ref[:, column(h, ref)]
        at = tokens
        for ref in got:
            size = ref.shape[1]
            keys[slot, at : at + size, :HDIM] = ref[0, :, column(h, ref)]
            vals[slot, at : at + size] = ref[1, :, column(h, ref)]
            at += size
        query = jnp.concatenate([q_ref[:, column(h, q_ref)], choose], axis=1)
        return dot(query, keys[slot], NT), dot(g_ref[:, column(h, g_ref)], vals[slot], NT)

    ahead = products(0)
    for h in range(heads):
        scores, dprob = ahead
        if h + 1 < heads:
            ahead = products(h + 1)
        scores = scores * (SCALE * LOG2E)
        weights = jnp.exp2(scores - jnp.max(scores, axis=1, keepdims=True))
        weights = weights * (1.0 / jnp.sum(weights, axis=1, keepdims=True))
        rounded = weights.astype(BF16)
        inner = jnp.sum(weights * dprob, axis=1, keepdims=True)
        dscore = (weights * (dprob - inner)).astype(BF16)
        slot = h % 2
        query, grad = q_ref[:, column(h, q_ref)], g_ref[:, column(h, g_ref)]
        o_ref[:, column(h, o_ref)] = dot(rounded, vals[slot]).astype(BF16)
        dq_ref[:, column(h, dq_ref)] = (dot(dscore, keys[slot, :, :HDIM]) * SCALE).astype(BF16)
        for side, term in enumerate((dot(dscore, query, TN) * SCALE, dot(rounded, grad, TN))):
            own_ref[side, :, column(h, own_ref)] = term[:tokens]
            at = tokens
            for ref in back:
                size = ref.shape[1]
                ref[side, :, column(h, ref)] = term[at : at + size].astype(BF16)
                at += size


def attend(mask, queries, out_grad, keys, values, got, rows, previous, head, heads):
    tokens, feat = queries.shape
    width = heads * HDIM
    sizes = [piece.shape[1] for piece in got]
    total = tokens + sum(sizes)
    inputs = vmem((queries, out_grad, keys, values, *got))
    aliases = {}
    if previous is not None:
        aliases = {1 + len(inputs): 0, 2 + len(inputs): 1}
        inputs += vmem(previous)
    whole = pl.BlockSpec(memory_space=pltpu.VMEM)
    out_shape = [pltpu.VMEM((tokens, feat), BF16)] * 2 + [pltpu.VMEM((2, tokens, width), F32)]
    out_shape += [pltpu.VMEM((2, size, width), BF16) for size in sizes]
    return pl.pallas_call(
        functools.partial(attend_kernel, head, heads, rows, len(aliases)),
        out_shape=out_shape,
        in_specs=[pl.BlockSpec(memory_space=pltpu.SMEM)] + [whole] * len(inputs),
        out_specs=[whole] * len(out_shape),
        scratch_shapes=[
            pltpu.VMEM((2, total, 2 * HDIM), BF16),
            pltpu.VMEM((2, total, HDIM), BF16),
        ],
        input_output_aliases=aliases,
        compiler_params=pltpu.CompilerParams(vmem_limit_bytes=24 << 20),
        cost_estimate=cost(
            12 * tokens * total * width,
            2 * width * (6 * tokens + 4 * tokens + 4 * (total - tokens)),
            tokens * total * heads,
        ),
    )(mask, *inputs)


def combine_kernel(head, heads, rows, aliased, pick_ref, own_ref, *refs):
    got = refs[: len(rows)]
    refs = refs[len(rows) + aliased :]
    outs, acc, done, sem = refs[:2], refs[2], refs[3], refs[4]
    tokens = own_ref.shape[1]
    starts = [[start_of(kind, pick_ref, tokens) for kind, _ in parts] for parts in rows]
    copies = []
    step = heads * HDIM // 2
    for side, at_col in ((side, col) for side in range(2) for col in (0, step)):
        cols = pl.ds(at_col, step)
        acc[:, cols] = own_ref[side, :, cols]
        for ref, parts, spots in zip(got, rows, starts, strict=True):
            at = 0
            whole = ref.shape[2] != heads * HDIM
            cut = pl.ds(at_col + (head * HDIM if whole else 0), step)
            for (_, size), start in zip(parts, spots, strict=True):
                acc[pl.ds(start, size), cols] += ref[side, at : at + size, cut].astype(F32)
                at += size
        done[side, :, cols] = acc[:, cols].astype(BF16)
        target = outs[side].at[:, pl.ds(head * HDIM + at_col, step)]
        copies.append(
            pltpu.make_async_copy(done.at[side, :, cols], target, sem.at[len(copies)])
        )
        copies[-1].start()
    for copy in copies:
        copy.wait()


def combine(picks, own, got, rows, previous, head, heads, feat):
    tokens = own.shape[1]
    inputs = vmem((own, *got))
    specs = [pl.BlockSpec(memory_space=pltpu.VMEM)] * len(inputs)
    aliases = {}
    if previous is not None:
        aliases = {1 + len(inputs): 0, 2 + len(inputs): 1}
        inputs += hbm(previous)
        specs += [ANY, ANY]
    return pl.pallas_call(
        functools.partial(combine_kernel, head, heads, rows, len(aliases)),
        out_shape=[pltpu.HBM((tokens, feat), BF16)] * 2,
        in_specs=[pl.BlockSpec(memory_space=pltpu.SMEM)] + specs,
        out_specs=[ANY, ANY],
        scratch_shapes=[
            pltpu.VMEM((tokens, heads * HDIM), F32),
            pltpu.VMEM((2, tokens, heads * HDIM), BF16),
            pltpu.SemaphoreType.DMA((4,)),
        ],
        input_output_aliases=aliases,
        compiler_params=pltpu.CompilerParams(vmem_limit_bytes=8 << 20),
        cost_estimate=cost(0, 8 * own.size),
    )(picks, *inputs)


def after(pieces, results):
    return [lax.optimization_barrier((piece, *results))[0] for piece in pieces]


def per_device(queries, key_rows, value_rows, out_grad, block_mask, block_pick):
    frames = lax.axis_size("frame")
    levels = frames.bit_length() - 1
    feat = queries.shape[1]
    mask = jnp.swapaxes(block_mask, 1, 2)
    rows = [[(level, BLK)] for level in range(levels - 1, 0, -1)]
    rows += [[(0, BLK), (PAIR, EDGE)], [(BEYOND, EDGE)]]
    pairs = [[(f, f ^ (1 << level)) for f in range(frames)] for level in range(levels - 1, -1, -1)]
    beyond = [f + (1 if f % 2 else -1) for f in range(frames)]
    pairs.append([(f, g if 0 <= g < frames else f) for f, g in enumerate(beyond)])

    def send(pieces, to):
        return [lax.ppermute(piece, "frame", t) for piece, t in zip(pieces, to, strict=True)]

    far = len(rows) - 2
    heads_at = [sum(SPLIT[:i]) for i in range(len(SPLIT))]
    chunks = list(zip(heads_at, SPLIT, strict=True))
    cuts = [[(parts, at * HDIM, n * HDIM) for parts in rows[:far]] for at, n in chunks]
    return_gates = [[]] * far + [[far], [*range(far + 1)]]

    def gated(pieces, before, gates):
        return [
            lax.optimization_barrier((piece, *(before[i] for i in gate)))[0]
            for piece, gate in zip(pieces, gates, strict=True)
        ]

    whole = [(rows[far], 0, feat), (rows[far + 1], 0, feat)]
    *near, = pack(block_pick, key_rows, value_rows, whole + cuts[0])
    first = near[2:]
    edge = send(near[1:2], pairs[far + 1 :])
    fetched = [send(first, pairs[:far])]
    near = send(near[:1], pairs[far : far + 1])
    last = first[:1]
    for cut in cuts[1:]:
        *pieces, = pack(block_pick, *after((key_rows, value_rows), last), cut)
        last = pieces[:1]
        before = fetched[-1]
        gates = [[before[0], *near] for i in range(far)]
        pieces = [after([p], gate)[0] for p, gate in zip(pieces, gates, strict=True)]
        fetched.append(send(pieces, pairs[:far]))
    fetched = [got + near + edge for got in fetched]
    outs = None
    returned = []
    for (head, heads), got in zip(chunks, fetched, strict=True):
        attended, query_grad, own, *terms = attend(
            mask, queries, out_grad, key_rows, value_rows, got, rows, outs, head, heads
        )
        outs = (attended, query_grad)
        if returned:
            terms = gated(terms, returned[-1][1], return_gates)
        returned.append((own, send(terms, pairs)))
    grads = None
    for (head, heads), (own, got) in zip(chunks, returned, strict=True):
        grads = combine(block_pick, own, got, rows, grads, head, heads, feat)
    return (*outs, *grads)


def solution(mesh):
    flat = P(("group", "frame"), None)
    return jax.shard_map(
        per_device,
        mesh=mesh,
        in_specs=(flat, flat, flat, flat, P(("group", "frame"), None, None), flat),
        out_specs=(flat, flat, flat, flat),
        check_vma=False,
    )
```

```python
import functools

import jax
import jax.numpy as jnp
from jax import lax
from jax.experimental import pallas as pl
from jax.experimental.pallas import tpu as pltpu
from jax.sharding import PartitionSpec as P

HDIM = 128
BLK = 128
EDGE = 64
SCALE = HDIM ** (-0.5)
LOG2E = 1.4426950408889634
MASKED = -1e30
SPLIT = (6, 6)
PAIR = -1
BEYOND = -2

F32 = jnp.float32
BF16 = jnp.bfloat16
ANY = pl.BlockSpec(memory_space=pl.ANY)
NT = (((1,), (1,)), ((), ()))
TN = (((0,), (0,)), ((), ()))


def dot(lhs, rhs, dims=(((1,), (0,)), ((), ()))):
    return lax.dot_general(lhs, rhs, dims, preferred_element_type=F32)


def hbm(arrays):
    return [pltpu.with_memory_space_constraint(x, pltpu.HBM) for x in arrays]


def vmem(arrays):
    return [pltpu.with_memory_space_constraint(x, pltpu.VMEM) for x in arrays]


def cost(flops, moved, exps=0):
    return pl.CostEstimate(flops=flops, bytes_accessed=moved, transcendentals=exps)


def start_of(kind, pick_ref, tokens):
    odd = lax.axis_index("frame") % 2
    if kind == PAIR:
        return pl.multiple_of((1 - odd) * (tokens - EDGE), EDGE)
    if kind == BEYOND:
        return pl.multiple_of(odd * (tokens - EDGE), EDGE)
    return pl.multiple_of(pick_ref[0, kind] * BLK, BLK)


def pack_kernel(pieces, pick_ref, k_ref, v_ref, *rest):
    outs, sem = rest[:-1], rest[-1]
    copies = []
    for out, (parts, col, width) in zip(outs, pieces, strict=True):
        at = 0
        for kind, size in parts:
            start = start_of(kind, pick_ref, k_ref.shape[0])
            for side, src in enumerate((k_ref, v_ref)):
                copies.append(
                    pltpu.make_async_copy(
                        src.at[pl.ds(start, size), pl.ds(col, width)],
                        out.at[side, pl.ds(at, size)],
                        sem.at[len(copies)],
                    )
                )
            at += size
    for copy in copies:
        copy.start()
    for copy in copies:
        copy.wait()


def pack(picks, keys, values, pieces):
    sizes = [sum(size for _, size in parts) for parts, _, _ in pieces]
    return pl.pallas_call(
        functools.partial(pack_kernel, pieces),
        out_shape=[
            pltpu.VMEM((2, size, width), BF16)
            for size, (_, _, width) in zip(sizes, pieces, strict=True)
        ],
        in_specs=[pl.BlockSpec(memory_space=pltpu.SMEM), ANY, ANY],
        out_specs=[ANY] * len(pieces),
        scratch_shapes=[pltpu.SemaphoreType.DMA((2 * sum(len(parts) for parts, _, _ in pieces),))],
        compiler_params=pltpu.CompilerParams(vmem_limit_bytes=1 << 20),
        cost_estimate=cost(
            0, sum(8 * size * width for size, (_, _, width) in zip(sizes, pieces, strict=True))
        ),
    )(picks, *hbm((keys, values)))


def bias_columns(mask_ref, tokens, blocks, rows):
    frame, frames = lax.axis_index("frame"), lax.axis_size("frame")
    lane = lax.broadcasted_iota(jnp.int32, (1, HDIM), 1)
    pieces = [jnp.zeros((tokens, HDIM), BF16)]
    for parts in rows:
        for kind, size in parts:
            row = jnp.zeros((1, HDIM), F32)
            for b in range(blocks):
                if kind == BEYOND:
                    seen = (frame > 0) & (frame < frames - 1)
                elif kind != PAIR:
                    seen = mask_ref[0, b, kind] > 0
                else:
                    continue
                row = jnp.where(lane == b, jnp.where(seen, 0.0, MASKED), row)
            pieces.append(jnp.broadcast_to(row, (size, HDIM)).astype(BF16))
    return jnp.concatenate(pieces, axis=0)


def attend_kernel(head, heads, rows, aliased, mask_ref, *refs):
    count = len(rows)
    q_ref, g_ref, k_ref, v_ref = refs[:4]
    got = refs[4 : 4 + count]
    refs = refs[4 + count + aliased :]
    o_ref, dq_ref, own_ref = refs[:3]
    back = refs[3 : 3 + count]
    keys, vals = refs[3 + count :]
    tokens = q_ref.shape[0]
    blocks = tokens // BLK
    bias = bias_columns(mask_ref, tokens, blocks, rows)
    for slot in range(2):
        keys[slot, :, HDIM:] = bias
    block = lax.broadcasted_iota(jnp.int32, (tokens, HDIM), 0) // BLK
    lane = lax.broadcasted_iota(jnp.int32, (tokens, HDIM), 1)
    choose = jnp.where(lane == block, 1.0, 0.0).astype(BF16)

    def column(h, ref):
        return pl.ds((h if ref.shape[-1] == heads * HDIM else head + h) * HDIM, HDIM)

    def products(h):
        at = 0
        slot = h % 2
        for ref in (k_ref, v_ref):
            half = keys.at[slot, :, :HDIM] if ref is k_ref else vals.at[slot]
            half[0:tokens] = ref[:, column(h, ref)]
        at = tokens
        for ref in got:
            size = ref.shape[1]
            keys[slot, at : at + size, :HDIM] = ref[0, :, column(h, ref)]
            vals[slot, at : at + size] = ref[1, :, column(h, ref)]
            at += size
        query = jnp.concatenate([q_ref[:, column(h, q_ref)], choose], axis=1)
        return dot(query, keys[slot], NT), dot(g_ref[:, column(h, g_ref)], vals[slot], NT)

    ahead = products(0)
    for h in range(heads):
        scores, dprob = ahead
        if h + 1 < heads:
            ahead = products(h + 1)
        scores = scores * (SCALE * LOG2E)
        weights = jnp.exp2(scores - jnp.max(scores, axis=1, keepdims=True))
        weights = weights * (1.0 / jnp.sum(weights, axis=1, keepdims=True))
        rounded = weights.astype(BF16)
        inner = jnp.sum(weights * dprob, axis=1, keepdims=True)
        dscore = (weights * (dprob - inner)).astype(BF16)
        slot = h % 2
        query, grad = q_ref[:, column(h, q_ref)], g_ref[:, column(h, g_ref)]
        o_ref[:, column(h, o_ref)] = dot(rounded, vals[slot]).astype(BF16)
        dq_ref[:, column(h, dq_ref)] = (dot(dscore, keys[slot, :, :HDIM]) * SCALE).astype(BF16)
        for side, term in enumerate((dot(dscore, query, TN) * SCALE, dot(rounded, grad, TN))):
            own_ref[side, :, column(h, own_ref)] = term[:tokens]
            at = tokens
            for ref in back:
                size = ref.shape[1]
                ref[side, :, column(h, ref)] = term[at : at + size].astype(BF16)
                at += size


def attend(mask, queries, out_grad, keys, values, got, rows, previous, head, heads):
    tokens, feat = queries.shape
    width = heads * HDIM
    sizes = [piece.shape[1] for piece in got]
    total = tokens + sum(sizes)
    inputs = vmem((queries, out_grad, keys, values, *got))
    aliases = {}
    if previous is not None:
        aliases = {1 + len(inputs): 0, 2 + len(inputs): 1}
        inputs += vmem(previous)
    whole = pl.BlockSpec(memory_space=pltpu.VMEM)
    out_shape = [pltpu.VMEM((tokens, feat), BF16)] * 2 + [pltpu.VMEM((2, tokens, width), F32)]
    out_shape += [pltpu.VMEM((2, size, width), BF16) for size in sizes]
    return pl.pallas_call(
        functools.partial(attend_kernel, head, heads, rows, len(aliases)),
        out_shape=out_shape,
        in_specs=[pl.BlockSpec(memory_space=pltpu.SMEM)] + [whole] * len(inputs),
        out_specs=[whole] * len(out_shape),
        scratch_shapes=[
            pltpu.VMEM((2, total, 2 * HDIM), BF16),
            pltpu.VMEM((2, total, HDIM), BF16),
        ],
        input_output_aliases=aliases,
        compiler_params=pltpu.CompilerParams(vmem_limit_bytes=24 << 20),
        cost_estimate=cost(
            12 * tokens * total * width,
            2 * width * (6 * tokens + 4 * tokens + 4 * (total - tokens)),
            tokens * total * heads,
        ),
    )(mask, *inputs)


def combine_kernel(head, heads, rows, aliased, pick_ref, own_ref, *refs):
    got = refs[: len(rows)]
    refs = refs[len(rows) + aliased :]
    outs, acc, done, sem = refs[:2], refs[2], refs[3], refs[4]
    tokens = own_ref.shape[1]
    starts = [[start_of(kind, pick_ref, tokens) for kind, _ in parts] for parts in rows]
    copies = []
    for side in range(2):
        acc[...] = own_ref[side]
        for ref, parts, spots in zip(got, rows, starts, strict=True):
            at = 0
            cut = slice(None) if ref.shape[2] == heads * HDIM else slice(head * HDIM, (head + heads) * HDIM)
            for (_, size), start in zip(parts, spots, strict=True):
                acc[pl.ds(start, size)] += ref[side, at : at + size, cut].astype(F32)
                at += size
        done[side] = acc[...].astype(BF16)
        target = outs[side].at[:, pl.ds(head * HDIM, heads * HDIM)]
        copies.append(pltpu.make_async_copy(done.at[side], target, sem.at[side]))
        copies[-1].start()
    for copy in copies:
        copy.wait()


def combine(picks, own, got, rows, previous, head, heads, feat):
    tokens = own.shape[1]
    inputs = vmem((own, *got))
    specs = [pl.BlockSpec(memory_space=pltpu.VMEM)] * len(inputs)
    aliases = {}
    if previous is not None:
        aliases = {1 + len(inputs): 0, 2 + len(inputs): 1}
        inputs += hbm(previous)
        specs += [ANY, ANY]
    return pl.pallas_call(
        functools.partial(combine_kernel, head, heads, rows, len(aliases)),
        out_shape=[pltpu.HBM((tokens, feat), BF16)] * 2,
        in_specs=[pl.BlockSpec(memory_space=pltpu.SMEM)] + specs,
        out_specs=[ANY, ANY],
        scratch_shapes=[
            pltpu.VMEM((tokens, heads * HDIM), F32),
            pltpu.VMEM((2, tokens, heads * HDIM), BF16),
            pltpu.SemaphoreType.DMA((2,)),
        ],
        input_output_aliases=aliases,
        compiler_params=pltpu.CompilerParams(vmem_limit_bytes=8 << 20),
        cost_estimate=cost(0, 8 * own.size),
    )(picks, *inputs)


def after(pieces, results):
    return [lax.optimization_barrier((piece, *results))[0] for piece in pieces]


def per_device(queries, key_rows, value_rows, out_grad, block_mask, block_pick):
    frames = lax.axis_size("frame")
    levels = frames.bit_length() - 1
    feat = queries.shape[1]
    mask = jnp.swapaxes(block_mask, 1, 2)
    rows = [[(level, BLK)] for level in range(levels - 1, 0, -1)]
    rows += [[(0, BLK), (PAIR, EDGE)], [(BEYOND, EDGE)]]
    pairs = [[(f, f ^ (1 << level)) for f in range(frames)] for level in range(levels - 1, -1, -1)]
    beyond = [f + (1 if f % 2 else -1) for f in range(frames)]
    pairs.append([(f, g if 0 <= g < frames else f) for f, g in enumerate(beyond)])

    def send(pieces, to):
        return [lax.ppermute(piece, "frame", t) for piece, t in zip(pieces, to, strict=True)]

    far = len(rows) - 2
    heads_at = [sum(SPLIT[:i]) for i in range(len(SPLIT))]
    chunks = list(zip(heads_at, SPLIT, strict=True))
    cuts = [[(parts, at * HDIM, n * HDIM) for parts in rows[:far]] for at, n in chunks]
    return_gates = [[]] * far + [[far], [*range(far + 1)]]

    def gated(pieces, before, gates):
        return [
            lax.optimization_barrier((piece, *(before[i] for i in gate)))[0]
            for piece, gate in zip(pieces, gates, strict=True)
        ]

    whole = [(rows[far], 0, feat), (rows[far + 1], 0, feat)]
    *near, = pack(block_pick, key_rows, value_rows, whole + cuts[0])
    first = near[2:]
    edge = send(near[1:2], pairs[far + 1 :])
    fetched = [send(first, pairs[:far])]
    near = send(near[:1], pairs[far : far + 1])
    last = first[:1]
    for cut in cuts[1:]:
        *pieces, = pack(block_pick, *after((key_rows, value_rows), last), cut)
        last = pieces[:1]
        before = fetched[-1]
        gates = [[before[0], *near]] * (far - 1) + [[before[far - 1], *near]]
        pieces = [after([p], gate)[0] for p, gate in zip(pieces, gates, strict=True)]
        fetched.append(send(pieces, pairs[:far]))
    fetched = [got + near + edge for got in fetched]
    outs = None
    returned = []
    for (head, heads), got in zip(chunks, fetched, strict=True):
        attended, query_grad, own, *terms = attend(
            mask, queries, out_grad, key_rows, value_rows, got, rows, outs, head, heads
        )
        outs = (attended, query_grad)
        if returned:
            terms = gated(terms, returned[-1][1], return_gates)
        returned.append((own, send(terms, pairs)))
    grads = None
    for (head, heads), (own, got) in zip(chunks, returned, strict=True):
        grads = combine(block_pick, own, got, rows, grads, head, heads, feat)
    return (*outs, *grads)


def solution(mesh):
    flat = P(("group", "frame"), None)
    return jax.shard_map(
        per_device,
        mesh=mesh,
        in_specs=(flat, flat, flat, flat, P(("group", "frame"), None, None), flat),
        out_specs=(flat, flat, flat, flat),
        check_vma=False,
    )
```
